32 devices in a mesh: dp: 8 (over z, y), tensor: 4 (over x, core).
Axes of the slice: x: 2, y: 2, z: 4, core: 2. Of those that a mesh axis runs over, the one named last changes fastest.
Arguments:
- tokens: bfloat16 [1024, 2048], P('dp'), may hold values from -6 to 6
- cotangent: bfloat16 [1024, 2048], P('dp'), may hold values from -6 to 6
- lengths: int32 [8, 4], P('dp'), may hold values from 1 to 96, 128 in all within a row
- owner_index: int32 [1024], P('dp'), may hold values from 0 to 1023, as said below
- arrival_index: int32 [1024], P('dp'), may hold values from 0 to 1023, as said below
- norm_gain_mixer: float32 [2048], replicated, may hold values from 0.5 to 1.5
- in_weight: bfloat16 [2048, 2, 4096], P(None, None, 'tensor'), may hold values from -0.125 to 0.125
- conv_weight: float32 [4, 4096], P(None, 'tensor'), may hold values from -3 to 3
- conv_bias: float32 [4096], P('tensor'), may hold values from -3 to 3
- xproj_weight: bfloat16 [4096, 160], P('tensor'), may hold values from -0.09375 to 0.09375
- dt_weight: bfloat16 [128, 4096], P(None, 'tensor'), may hold values from -0.5 to 0.5
- dt_bias: float32 [4096], P('tensor'), may hold values from -6.5 to -2.5
- a_log: float32 [16, 4096], P(None, 'tensor'), may hold values from 0 to 2.77
- skip_gain: float32 [4096], P('tensor'), may hold values from 0.5 to 1.5
- out_weight: bfloat16 [4096, 2048], P('tensor'), may hold values from -0.1875 to 0.1875
- norm_gain_mlp: float32 [2048], replicated, may hold values from 0.5 to 1.5
- gate_up_weight: bfloat16 [2048, 2, 8192], P(None, None, 'tensor'), may hold values from -0.125 to 0.125
- down_weight: bfloat16 [8192, 2048], P('tensor'), may hold values from -0.125 to 0.125
Outputs:
- output: bfloat16 [1024, 2048], P('dp')
- tokens_grad: bfloat16 [1024, 2048], P('dp')
- norm_gain_mixer_grad: float32 [2048], P('dp')
- in_weight_grad: float32 [2048, 2, 4096], P('dp', None, 'tensor')
- conv_weight_grad: float32 [4, 4096], P(None, ('tensor', 'dp'))
- conv_bias_grad: float32 [4096], P(('tensor', 'dp'))
- xproj_weight_grad: float32 [4096, 160], P(('tensor', 'dp'))
- dt_weight_grad: float32 [128, 4096], P('dp', 'tensor')
- dt_bias_grad: float32 [4096], P(('tensor', 'dp'))
- a_log_grad: float32 [16, 4096], P(None, ('tensor', 'dp'))
- skip_gain_grad: float32 [4096], P(('tensor', 'dp'))
- out_weight_grad: float32 [4096, 2048], P('tensor', 'dp')
- norm_gain_mlp_grad: float32 [2048], P('dp')
- gate_up_weight_grad: float32 [2048, 2, 8192], P('dp', None, 'tensor')
- down_weight_grad: float32 [8192, 2048], P('tensor', 'dp')
The draws below stay inside these ranges and needn't reach their ends.
Inputs may be any that keep to these rules, and one draw needn't show every extreme that they name: `owner_index`: A permutation of the 1024 places; the 128 tokens of each index of dp go in exactly 16 to each block of 128 places of the owners' layout. `arrival_index`: the inverse permutation of owner_index. `lengths`: each row sums to 128, and its largest entry is 96.
All inputs are finite; a program needn't handle non-finite values.
Results may differ from the reference program's by a relative error of at most 0.015.
Values may be sent and summed in bfloat16 or wider, within the bound.
A program may use at most 384 MiB of HBM per device.

```python
import math
import jax
import jax.numpy as jnp
import numpy as np
from jax import lax

D = 2048
DI = 4096
N = 16
CONV = 4
R = 128
FF = 8192
SEQ_DEV = 4
TOK_DEV = 128
MOST = 96
TOKENS = 1024
N_DP = 8


def index_tables(key):
    folded = jax.random.fold_in(key, 17)
    group_count = TOKENS // TOK_DEV
    share_rows = TOK_DEV // group_count
    slot_key, row_key = jax.random.split(folded)
    slot_perm = jax.vmap(lambda subkey: jax.random.permutation(subkey, TOK_DEV))(jax.random.split(slot_key, group_count))
    row_perm = jax.vmap(lambda subkey: jax.random.permutation(subkey, TOK_DEV))(jax.random.split(row_key, group_count))
    row_place = jnp.argsort(row_perm, axis=1).astype(jnp.int32)
    source = (slot_perm // share_rows).astype(jnp.int32)
    within = (slot_perm % share_rows).astype(jnp.int32)
    target = jnp.arange(group_count, dtype=jnp.int32)[:, None]
    arrival_row = row_place[source, target * share_rows + within]
    arrival_rows = (source * TOK_DEV + arrival_row).reshape(-1).astype(jnp.int32)
    owner_rows = jnp.argsort(arrival_rows).astype(jnp.int32)
    return (owner_rows, arrival_rows)


def draw_owner_index(key, part):
    return index_tables(key)[0]


def draw_arrival_index(key, part):
    return index_tables(key)[1]


def with_spikes(array, own_key, source, target, shards_of, factor):
    owner, partner = [(jnp.arange(array.shape[axis_at]) // (array.shape[axis_at] // shards_of)).reshape([-1 if axis == axis_at else 1 for axis in range(array.ndim)]) for axis_at in (source, target)]
    chosen = jax.random.permutation(own_key, shards_of)[partner]
    strong = (owner == chosen) | (owner == (partner + shards_of // 2) % shards_of)
    return jnp.where(strong, factor * array, array)


def steps_of(rng, extent, cuts, low, largest):
    level = 1.0
    for axis_at, parts in cuts:
        draws = jax.random.uniform(jax.random.fold_in(jax.random.fold_in(rng, 6), axis_at), (parts,), jnp.float32, low / len(cuts), largest / len(cuts))
        level = level * jnp.repeat(jnp.exp(draws), extent[axis_at] // parts).reshape((-1,) + (1,) * (len(extent) - 1 - axis_at))
    return level


def length_profile(count, total, bound, lean):
    loads = [(1 << 20) // math.isqrt(grade ** lean) + 1 for grade in range(2, count + 1)]
    spare, given = total - bound - (count - 1), [1] * (count - 1)
    while spare > 0:
        movable = [i for i in range(count - 1) if given[i] < bound]
        whole, remaining = sum([loads[i] for i in movable]), spare
        for i in movable:
            more = min(bound - given[i], max(1, remaining * loads[i] // whole), spare)
            given[i] = given[i] + more
            spare = spare - more
    return np.array([bound] + given)


def uneven(key, number_of, total, reach, skew):
    if number_of == 2:
        one = jax.random.randint(key, (), max(1, total - reach), min(reach, total - 1) + 1)
        return jnp.stack([one, total - one])
    sizes = jnp.asarray(length_profile(number_of, total, reach, skew), jnp.int32)
    twos = (number_of - 1) // 2
    source_of, sink = sizes[1:1 + 2 * twos:2], sizes[2:2 + 2 * twos:2]
    slack = jnp.minimum(source_of - 1, reach - sink)
    shifted = jax.random.randint(jax.random.fold_in(key, 1), (twos,), 0, 1 << 20) % (slack + 1)
    sizes = sizes.at[1:1 + 2 * twos:2].set(source_of - shifted).at[2:2 + 2 * twos:2].set(sink + shifted)
    return sizes[jax.random.permutation(jax.random.fold_in(key, 2), number_of)]


def centred(own_key, extent, scale, most, shards=(), kind=jnp.bfloat16):
    level = steps_of(own_key, extent, shards, -0.22, 0.18) if shards else 1.0
    drawn = jax.random.normal(own_key, extent, jnp.float32) * scale * level
    return jnp.minimum(jnp.maximum(drawn, -most), most).astype(kind)


def noise_with(rng, extent, width, bound, cuts, heavy, kind=jnp.bfloat16):
    entries = width * jax.random.normal(rng, extent, jnp.float32)
    if cuts:
        entries = entries * steps_of(rng, extent, cuts, -0.22, 0.18)
    return jnp.clip(with_spikes(entries, jax.random.fold_in(rng, 3), *heavy), -bound, bound).astype(kind)


def setup_inputs(seed: int = 0) -> dict:
    key_list = jax.random.split(jax.random.key(seed), 19)
    tokens = centred(key_list[0], (TOKENS, D), 1.0, 6.0, ((0, 8),))
    cotangent = noise_with(key_list[1], (TOKENS, D), 1.0, 6.0, ((0, 8),), (0, 1, 8, 2.0))
    lengths = jax.vmap(lambda own: uneven(own, SEQ_DEV, TOK_DEV, MOST, 1))(jax.random.split(key_list[2], N_DP)).reshape((N_DP, SEQ_DEV)).astype(jnp.int32)
    owner_index = draw_owner_index(jax.random.fold_in(key_list[18], 71), 0)
    arrival_index = draw_arrival_index(jax.random.fold_in(key_list[18], 71), 0)
    norm_gain_mixer = jnp.clip(1.0 + 0.1 * jax.random.normal(key_list[5], (D,), jnp.float32), 0.5, 1.5)
    in_weight = centred(key_list[6], (D, 2, DI), D ** -0.5, 0.125, ((2, 4),))
    conv_weight = centred(key_list[7], (CONV, DI), CONV ** -0.5, 3.0, ((1, 4),), jnp.float32)
    conv_bias = centred(key_list[8], (DI,), 0.5, 3.0, ((0, 4),), jnp.float32)
    xproj_weight = centred(key_list[9], (DI, R + 2 * N), DI ** -0.5, 0.09375, ((0, 4),))
    dt_weight = centred(key_list[10], (R, DI), R ** -0.5, 0.5, ((1, 4),))
    dt_bias = jnp.clip(-6.5 + 4.0 * jax.random.uniform(key_list[11], (DI,), jnp.float32) ** steps_of(key_list[11], (DI,), ((0, 4),), -0.2, 0.2), -6.5, -2.5)
    a_log = jnp.clip(2.77 * jax.random.uniform(key_list[12], (N, DI), jnp.float32) ** steps_of(key_list[12], (N, DI), ((1, 4),), -0.2, 0.2), 0.0, 2.77)
    skip_gain = jnp.clip(0.5 + 1.0 * jax.random.uniform(key_list[13], (DI,), jnp.float32) ** steps_of(key_list[13], (DI,), ((0, 4),), -0.2, 0.2), 0.5, 1.5)
    out_weight = centred(key_list[14], (DI, D), (DI // 4) ** -0.5, 0.1875, ((0, 4),))
    norm_gain_mlp = jnp.clip(1.0 + 0.1 * jax.random.normal(key_list[15], (D,), jnp.float32), 0.5, 1.5)
    gate_up_weight = centred(key_list[16], (D, 2, FF), D ** -0.5, 0.125, ((2, 4),))
    down_weight = centred(key_list[17], (FF, D), (FF // 4) ** -0.5, 0.125, ((0, 4),))
    return {"tokens": tokens, "cotangent": cotangent, "lengths": lengths, "owner_index": owner_index, "arrival_index": arrival_index, "norm_gain_mixer": norm_gain_mixer, "in_weight": in_weight, "conv_weight": conv_weight, "conv_bias": conv_bias, "xproj_weight": xproj_weight, "dt_weight": dt_weight, "dt_bias": dt_bias, "a_log": a_log, "skip_gain": skip_gain, "out_weight": out_weight, "norm_gain_mlp": norm_gain_mlp, "gate_up_weight": gate_up_weight, "down_weight": down_weight}


EPS = 1e-05
highest = lax.Precision.HIGHEST

@jax.custom_vjp
def low(v):
    return lax.optimization_barrier(v.astype(jnp.bfloat16)).astype(jnp.float32)

@jax.custom_vjp
def low_back(v):
    return v

def low_keep(v):
    return (low(v), None)

def low_pass(kept, grad):
    return (grad,)

def back_keep(v):
    return (v, None)

def back_low(kept, grad):
    return (low(grad),)
low.defvjp(low_keep, low_pass)
low_back.defvjp(back_keep, back_low)

def product(left, right):
    return jnp.dot(left, right, precision=highest, preferred_element_type=jnp.float32)

def rms_scale(values):
    return lax.rsqrt(lax.optimization_barrier(jnp.mean(values * values, axis=-1, keepdims=True)) + EPS)

def sequence_offsets(lengths_row, row_count):
    starts = (jnp.cumsum(lengths_row) - lengths_row).astype(jnp.int32)
    positions = jnp.arange(row_count, dtype=jnp.int32)
    begins = lax.optimization_barrier(jnp.max(jnp.where(starts[None, :] <= positions[:, None], starts[None, :], 0), axis=1))
    return (positions - begins).astype(jnp.int32)

def shift_down(values, amount):
    if amount == 0:
        return values
    padding = jnp.zeros((amount,) + values.shape[1:], values.dtype)
    return jnp.concatenate([padding, values[:-amount]], axis=0)

def causal_conv(inner_part, weight, conv_bias, offset):
    conv_taps = weight.shape[0]
    summed = conv_bias[None, :] + weight[conv_taps - 1][None, :] * inner_part
    for distance in range(1, conv_taps):
        valid_rows = (offset >= distance).astype(jnp.float32)[:, None]
        summed = summed + weight[conv_taps - 1 - distance][None, :] * shift_down(inner_part, distance) * valid_rows
    return summed

def combine(first_pair, second_pair):
    return (first_pair[0] * second_pair[0], second_pair[0] * first_pair[1] + second_pair[1])

def block_terms(step_size, b_proj, conv_in, keep_mask, decay_rate):
    factor = jnp.exp(step_size[:, None, :] * decay_rate[None, :, :]) * keep_mask[:, None, None]
    source = step_size[:, None, :] * b_proj[:, :, None] * conv_in[:, None, :]
    return (factor, source)

def to_blocks(values, block_count):
    return values.reshape((block_count, values.shape[0] // block_count) + values.shape[1:])

def selective_scan(step_size, b_proj, c_proj, conv_in, keep_mask, decay_rate):
    row_count = step_size.shape[0]
    block_count = row_count // min(64, row_count)

    def advance(carried, pieces):
        block_step, block_b, block_c, block_conv, block_keep = pieces
        factor, source = block_terms(block_step, block_b, block_conv, block_keep, decay_rate)
        cumulative, partial_state = lax.associative_scan(combine, (factor, source), axis=0)
        states = cumulative * carried[None] + partial_state
        result = jnp.einsum('tn,tnc->tc', block_c, states, precision=highest)
        return (states[-1], result)
    initial = jnp.zeros(decay_rate.shape, jnp.float32)
    pieces = tuple((to_blocks(values, block_count) for values in (step_size, b_proj, c_proj, conv_in, keep_mask)))
    leftover, results = lax.scan(jax.checkpoint(advance), initial, pieces)
    return results.reshape(row_count, -1)

def block_forward(owned_rows, offset, norm_gain_mixer, in_weight, conv_weight, conv_bias, xproj_weight, dt_weight, dt_bias, a_log, skip_gain, out_weight, norm_gain_mlp, gate_up_weight, down_weight):
    normed = low(owned_rows * rms_scale(owned_rows) * norm_gain_mixer)
    projected = low_back(product(normed, in_weight.reshape(D, 2 * DI)))
    inner_part = projected[:, :DI]
    gate_z = projected[:, DI:]
    conv_out = low(jax.nn.silu(causal_conv(inner_part, conv_weight, conv_bias, offset)))
    pieces = low_back(product(conv_out, xproj_weight))
    dt_low = low(pieces[:, :R])
    b_proj = pieces[:, R:R + N]
    c_proj = pieces[:, R + N:]
    step_size = jax.nn.softplus(low_back(product(dt_low, dt_weight)) + dt_bias)
    decay_rate = -jnp.exp(a_log)
    keep_mask = (offset > 0).astype(jnp.float32)
    scanned = selective_scan(step_size, b_proj, c_proj, conv_out, keep_mask, decay_rate) + skip_gain * conv_out
    gated = low(scanned * jax.nn.silu(gate_z))
    mixer_out = low_back(product(gated, out_weight))
    hidden_in = owned_rows + mixer_out
    normed_mlp = low(hidden_in * rms_scale(hidden_in) * norm_gain_mlp)
    gate_up = low_back(product(normed_mlp, gate_up_weight.reshape(D, 2 * FF)))
    hidden = low(jax.nn.silu(gate_up[:, :FF]) * gate_up[:, FF:])
    return hidden_in + low_back(product(hidden, down_weight))

def reference(tokens, cotangent, lengths, owner_index, arrival_index, norm_gain_mixer, in_weight, conv_weight, conv_bias, xproj_weight, dt_weight, dt_bias, a_log, skip_gain, out_weight, norm_gain_mlp, gate_up_weight, down_weight):
    weights = tuple((values.astype(jnp.float32) for values in (norm_gain_mixer, in_weight, conv_weight, conv_bias, xproj_weight, dt_weight, dt_bias, a_log, skip_gain, out_weight, norm_gain_mlp, gate_up_weight, down_weight)))
    offsets = jax.vmap(lambda lengths_row: sequence_offsets(lengths_row, TOK_DEV))(lengths)

    def forward(tokens_in, *weight_list):
        owners = tokens_in[arrival_index].reshape(N_DP, TOK_DEV, D)

        def per_block(carried, pieces):
            return (carried, block_forward(pieces[0], pieces[1], *weight_list))
        leftover, outputs = lax.scan(jax.checkpoint(per_block), jnp.zeros((), jnp.float32), (owners, offsets))
        return outputs.reshape(TOKENS, D)[owner_index]
    output, pullback = jax.vjp(forward, tokens.astype(jnp.float32), *weights)
    gradients = pullback(cotangent.astype(jnp.float32))
    return (output.astype(jnp.bfloat16), gradients[0].astype(jnp.bfloat16), gradients[1], gradients[2], gradients[3], gradients[4], gradients[5], gradients[6], gradients[7], gradients[8], gradients[9], gradients[10], gradients[11], gradients[12], gradients[13])
```

```python
import functools

import jax
import jax.numpy as jnp
from jax import lax
from jax.experimental import pallas as pl
from jax.experimental.pallas import tpu as pltpu
from jax.sharding import PartitionSpec as P

EPS = 1e-05
LOG2E = 1.4426950408889634
LANES = 128
ROWS = 16
GROUP = 8


def rms_scale(values):
    return lax.rsqrt(jnp.mean(values * values, axis=-1, keepdims=True) + EPS)


def rms_back(upstream, values, row_scale):
    return row_scale * (
        upstream
        - values * row_scale * row_scale * jnp.mean(upstream * values, axis=-1, keepdims=True)
    )


def silu_slope(values):
    logistic = jax.nn.sigmoid(values)
    return logistic * (1.0 + values * (1.0 - logistic))


def sequence_offsets(lengths_row, row_count):
    starts = jnp.cumsum(lengths_row) - lengths_row
    positions = jnp.arange(row_count, dtype=jnp.int32)
    begins = jnp.max(jnp.where(starts[None, :] <= positions[:, None], starts[None, :], 0), axis=1)
    return positions - begins


def shift_down(values, amount):
    if amount == 0:
        return values
    padding = jnp.zeros((amount,) + values.shape[1:], values.dtype)
    return jnp.concatenate([padding, values[:-amount]], axis=0)


def shift_up(values, amount):
    if amount == 0:
        return values
    padding = jnp.zeros((amount,) + values.shape[1:], values.dtype)
    return jnp.concatenate([values[amount:], padding], axis=0)


def causal_conv(inner_part, weight, conv_bias, offset):
    conv_taps = weight.shape[0]
    summed = conv_bias[None, :] + weight[conv_taps - 1][None, :] * inner_part
    for distance in range(1, conv_taps):
        valid_rows = (offset >= distance).astype(jnp.float32)[:, None]
        summed = (
            summed
            + weight[conv_taps - 1 - distance][None, :]
            * shift_down(inner_part, distance)
            * valid_rows
        )
    return summed


def scan_fwd_kernel(keep_ref, step_ref, u_ref, rate_ref, b_ref, c_ref, states_ref, y_ref, state_ref):
    width = step_ref.shape[1]
    spread = rate_ref.shape[0]
    block = pl.program_id(0)

    @pl.when(block == 0)
    def _():
        state_ref[...] = jnp.zeros_like(state_ref)

    tiles = width // LANES
    slices = [pl.ds(j * LANES, LANES) for j in range(tiles)]

    mine = lax.broadcasted_iota(jnp.int32, (GROUP, LANES), 0)

    def wide(ref, base, r, j):
        tile = ref[pl.ds(base, GROUP), slices[j]]
        return jnp.broadcast_to(tile[r : r + 1], (spread, LANES))

    def group(k, state):
        base = pl.multiple_of(k * GROUP, GROUP)
        state = list(state)
        y = [jnp.zeros((GROUP, LANES), jnp.float32)] * tiles
        for r in range(GROUP):
            keep = keep_ref[block * ROWS + base + r]
            b_row = b_ref[base + r]
            c_row = c_ref[base + r]
            for j in range(tiles):
                step = wide(step_ref, base, r, j)
                u = wide(u_ref, base, r, j)
                factor = jnp.exp2(step * rate_ref[:, slices[j]]) * keep
                state[j] = factor * state[j] + u * b_row
                states_ref[base + r, :, slices[j]] = state[j]
                y[j] = jnp.where(mine == r, jnp.sum(c_row * state[j], axis=0, keepdims=True), y[j])
        for j in range(tiles):
            y_ref[pl.ds(base, GROUP), slices[j]] = y[j]
        return tuple(state)

    state = tuple(state_ref[:, s] for s in slices)
    state = lax.fori_loop(0, ROWS // GROUP, group, state)
    for j in range(tiles):
        state_ref[:, slices[j]] = state[j]


def scan_fwd(keep, step_size, u, rate2, b_wide, c_wide):
    rows, width = step_size.shape
    n = rate2.shape[0]
    row_spec = pl.BlockSpec((ROWS, width), lambda i: (i, 0))
    wide_spec = pl.BlockSpec((ROWS, n, LANES), lambda i: (i, 0, 0))
    return pl.pallas_call(
        scan_fwd_kernel,
        grid=(rows // ROWS,),
        in_specs=[
            pl.BlockSpec(memory_space=pltpu.SMEM),
            row_spec,
            row_spec,
            pl.BlockSpec((n, width), lambda i: (0, 0)),
            wide_spec,
            wide_spec,
        ],
        out_specs=[pl.BlockSpec((ROWS, n, width), lambda i: (i, 0, 0)), row_spec],
        out_shape=[
            jax.ShapeDtypeStruct((rows, n, width), jnp.float32),
            jax.ShapeDtypeStruct((rows, width), jnp.float32),
        ],
        scratch_shapes=[pltpu.VMEM((n, width), jnp.float32)],
        name="scan_fwd",
    )(keep, step_size, u, rate2, b_wide, c_wide)


def scan_bwd_kernel(
    keep_ref,
    step_ref,
    conv_ref,
    ds_ref,
    rate_ref,
    b_ref,
    c_ref,
    states_ref,
    before_ref,
    d_step_ref,
    g_ref,
    db_ref,
    dc_ref,
    decay_ref,
    carry_ref,
):
    width = step_ref.shape[1]
    spread = rate_ref.shape[0]
    index = pl.program_id(0)
    block = pl.num_programs(0) - 1 - index

    @pl.when(index == 0)
    def _():
        carry_ref[...] = jnp.zeros_like(carry_ref)
        decay_ref[...] = jnp.zeros_like(decay_ref)

    tiles = width // LANES
    slices = [pl.ds(j * LANES, LANES) for j in range(tiles)]

    mine = lax.broadcasted_iota(jnp.int32, (GROUP, LANES), 0)

    def wide(ref, base, r, j):
        tile = ref[pl.ds(base, GROUP), slices[j]]
        return jnp.broadcast_to(tile[r : r + 1], (spread, LANES))

    def group(k, carry):
        base = pl.multiple_of(ROWS - GROUP - k * GROUP, GROUP)
        carry = list(carry)
        zero = jnp.zeros((GROUP, LANES), jnp.float32)
        d_step, weighted = [zero] * tiles, [zero] * tiles
        for r in reversed(range(GROUP)):
            t = base + r
            keep = keep_ref[block * ROWS + t]
            b_row = b_ref[t]
            c_row = c_ref[t]
            db = jnp.zeros((spread, LANES), jnp.float32)
            dc = jnp.zeros((spread, LANES), jnp.float32)
            for j in range(tiles):
                step = wide(step_ref, base, r, j)
                conv = wide(conv_ref, base, r, j)
                ds = wide(ds_ref, base, r, j)
                rate = rate_ref[:, slices[j]]
                factor = jnp.exp2(step * (rate * LOG2E)) * keep
                grad = c_row * ds + carry[j]
                passed = factor * grad
                if r == 0:
                    previous = jnp.where(
                        base == 0,
                        before_ref[0, :, slices[j]],
                        states_ref[jnp.maximum(t - 1, 0), :, slices[j]],
                    )
                else:
                    previous = states_ref[t - 1, :, slices[j]]
                via = passed * previous
                g = jnp.sum(grad * b_row, axis=0, keepdims=True)
                through = jnp.sum(via * rate, axis=0, keepdims=True) + conv[:1] * g
                d_step[j] = jnp.where(mine == r, through, d_step[j])
                weighted[j] = jnp.where(mine == r, g, weighted[j])
                decay_ref[:, slices[j]] += via * step
                db = db + grad * (step * conv)
                dc = dc + states_ref[t, :, slices[j]] * ds
                carry[j] = passed
            db_ref[t] = db
            dc_ref[t] = dc
        for j in range(tiles):
            d_step_ref[pl.ds(base, GROUP), slices[j]] = d_step[j]
            g_ref[pl.ds(base, GROUP), slices[j]] = weighted[j]
        return tuple(carry)

    carry = tuple(carry_ref[:, s] for s in slices)
    carry = lax.fori_loop(0, ROWS // GROUP, group, carry)
    for j in range(tiles):
        carry_ref[:, slices[j]] = carry[j]


def scan_bwd(keep, step_size, conv_in, d_scanned, rate, b_wide, c_wide, states):
    rows, width = step_size.shape
    n = rate.shape[0]
    last = rows // ROWS - 1
    row_spec = pl.BlockSpec((ROWS, width), lambda i: (last - i, 0))
    wide_spec = pl.BlockSpec((ROWS, n, LANES), lambda i: (last - i, 0, 0))
    return pl.pallas_call(
        scan_bwd_kernel,
        grid=(rows // ROWS,),
        in_specs=[
            pl.BlockSpec(memory_space=pltpu.SMEM),
            row_spec,
            row_spec,
            row_spec,
            pl.BlockSpec((n, width), lambda i: (0, 0)),
            wide_spec,
            wide_spec,
            pl.BlockSpec((ROWS, n, width), lambda i: (last - i, 0, 0)),
            pl.BlockSpec((1, n, width), lambda i: (jnp.maximum((last - i) * ROWS - 1, 0), 0, 0)),
        ],
        out_specs=[
            row_spec,
            row_spec,
            wide_spec,
            wide_spec,
            pl.BlockSpec((n, width), lambda i: (0, 0)),
        ],
        out_shape=[
            jax.ShapeDtypeStruct((rows, width), jnp.float32),
            jax.ShapeDtypeStruct((rows, width), jnp.float32),
            jax.ShapeDtypeStruct((rows, n, LANES), jnp.float32),
            jax.ShapeDtypeStruct((rows, n, LANES), jnp.float32),
            jax.ShapeDtypeStruct((n, width), jnp.float32),
        ],
        scratch_shapes=[pltpu.VMEM((n, width), jnp.float32)],
        name="scan_bwd",
    )(keep, step_size, conv_in, d_scanned, rate, b_wide, c_wide, states, states)


def one_hot_rows(places, count):
    return (jnp.arange(count, dtype=jnp.int32)[:, None] == places[None, :]).astype(jnp.bfloat16)


def rank_within(values):
    return jnp.sum((values[None, :] < values[:, None]).astype(jnp.int32), axis=1)


def slots_of(index, row_count, share):
    peer = index // row_count
    rows = jnp.arange(row_count, dtype=jnp.int32)
    earlier = (peer[None, :] == peer[:, None]) & (rows[None, :] < rows[:, None])
    return peer * share + jnp.sum(earlier.astype(jnp.int32), axis=1)


def pick_rows(selector, values):
    return jnp.dot(selector, values, preferred_element_type=jnp.float32).astype(jnp.bfloat16)


def body(
    tokens,
    cotangent,
    lengths,
    owner_index,
    arrival_index,
    norm_gain_mixer,
    in_weight,
    conv_weight,
    conv_bias,
    xproj_weight,
    dt_weight,
    dt_bias,
    a_log,
    skip_gain,
    out_weight,
    norm_gain_mlp,
    gate_up_weight,
    down_weight,
    *,
    n_dp,
):
    row_count, model_width = tokens.shape
    inner_width = in_weight.shape[2]
    hidden_width = gate_up_weight.shape[2]
    rank_width = dt_weight.shape[0]
    state_width = a_log.shape[0]
    share = row_count // n_dp
    me = lax.axis_index("dp")

    def exchange(values):
        return lax.all_to_all(values, "dp", split_axis=0, concat_axis=0, tiled=True)

    def columns_for_all(values):
        return lax.all_to_all(values, "dp", split_axis=1, concat_axis=0, tiled=True)

    def gather_rows(values):
        return lax.all_gather(values, "dp", axis=0, tiled=True)

    send_select = one_hot_rows(rank_within(owner_index), row_count)
    owner_slots = slots_of(arrival_index, row_count, share)
    take_select = jnp.transpose(one_hot_rows(owner_slots, row_count))
    owned_bf16 = pick_rows(take_select, exchange(pick_rows(send_select, tokens)))
    owned_grad = pick_rows(take_select, exchange(pick_rows(send_select, cotangent)))
    grad_all = gather_rows(owned_grad)
    owned_rows = owned_bf16.astype(jnp.float32)
    offset = sequence_offsets(lengths[0], row_count)
    keep_mask = (offset > 0).astype(jnp.float32)
    scale_mixer = rms_scale(owned_rows)
    normed = (owned_rows * scale_mixer * norm_gain_mixer).astype(jnp.bfloat16)
    normed_cols = columns_for_all(normed)
    in_flat = in_weight.reshape(model_width, 2 * inner_width)
    projected = jnp.dot(normed, in_flat, preferred_element_type=jnp.float32)
    inner_part = projected[:, :inner_width]
    gate_z = projected[:, inner_width:]
    conv_pre = causal_conv(inner_part, conv_weight, conv_bias, offset)
    conv_out = jax.nn.silu(conv_pre).astype(jnp.bfloat16)
    conv_in = conv_out.astype(jnp.float32)
    pieces = lax.psum(jnp.dot(conv_out, xproj_weight, preferred_element_type=jnp.float32), "tensor")
    dt_low = pieces[:, :rank_width].astype(jnp.bfloat16)
    b_proj = pieces[:, rank_width : rank_width + state_width]
    c_proj = pieces[:, rank_width + state_width :]
    b_wide = jnp.broadcast_to(b_proj[:, :, None], (row_count, state_width, LANES))
    c_wide = jnp.broadcast_to(c_proj[:, :, None], (row_count, state_width, LANES))
    dt_pre = jnp.dot(dt_low, dt_weight, preferred_element_type=jnp.float32) + dt_bias
    step_size = jax.nn.softplus(dt_pre)
    decay_rate = -jnp.exp(a_log)
    states, scan_part = scan_fwd(
        keep_mask, step_size, step_size * conv_in, decay_rate * LOG2E, b_wide, c_wide
    )
    scanned = scan_part + skip_gain * conv_in
    silu_z = jax.nn.silu(gate_z)
    gated = (scanned * silu_z).astype(jnp.bfloat16)
    gated_all = gather_rows(gated)
    mixer_out = lax.psum(jnp.dot(gated, out_weight, preferred_element_type=jnp.float32), "tensor")
    hidden_in = owned_rows + mixer_out
    scale_mlp = rms_scale(hidden_in)
    normed_mlp = (hidden_in * scale_mlp * norm_gain_mlp).astype(jnp.bfloat16)
    gate_flat = gate_up_weight.reshape(model_width, 2 * hidden_width)

    def mlp_parts(rows, grads):
        gate_up = jnp.dot(rows, gate_flat, preferred_element_type=jnp.float32)
        gate_part = gate_up[:, :hidden_width]
        up_part = gate_up[:, hidden_width:]
        hidden = (jax.nn.silu(gate_part) * up_part).astype(jnp.bfloat16)
        d_hidden = jnp.einsum("td,fd->tf", grads, down_weight, preferred_element_type=jnp.float32)
        d_gate = d_hidden * up_part * silu_slope(gate_part)
        d_up = d_hidden * jax.nn.silu(gate_part)
        return hidden, d_gate.astype(jnp.bfloat16), d_up.astype(jnp.bfloat16)

    hidden, d_gate, d_up = mlp_parts(normed_mlp, owned_grad)
    d_gate_up = jnp.concatenate([d_gate, d_up], axis=1)
    d_normed_mlp = lax.psum(
        jnp.einsum("tk,dk->td", d_gate_up, gate_flat, preferred_element_type=jnp.float32), "tensor"
    )
    normed_mlp_all = gather_rows(normed_mlp)
    down_out = lax.psum(jnp.dot(hidden, down_weight, preferred_element_type=jnp.float32), "tensor")
    output_own = (hidden_in + down_out).astype(jnp.bfloat16)
    upstream = owned_grad.astype(jnp.float32)
    gain_mlp_grad = jnp.sum(d_normed_mlp * hidden_in * scale_mlp, axis=0)
    d_hidden_in = upstream + rms_back(d_normed_mlp * norm_gain_mlp, hidden_in, scale_mlp)
    d_mixed = d_hidden_in.astype(jnp.bfloat16)
    d_mixed_cols = columns_for_all(d_mixed)
    d_gated = jnp.einsum("td,cd->tc", d_mixed, out_weight, preferred_element_type=jnp.float32)
    d_scanned = d_gated * silu_z
    d_gate_z = d_gated * scanned * silu_slope(gate_z)
    skip_grad = jnp.sum(d_scanned * conv_in, axis=0)
    d_step, b_weighted, db_part, dc_part, decay_grad = scan_bwd(
        keep_mask, step_size, conv_in, d_scanned, decay_rate, b_wide, c_wide, states
    )
    a_log_grad = decay_grad * decay_rate
    d_dt_pre = d_step * jax.nn.sigmoid(dt_pre)
    dt_bias_grad = jnp.sum(d_dt_pre, axis=0)
    d_dt_rounded = d_dt_pre.astype(jnp.bfloat16)
    dt_weight_grad = jnp.einsum(
        "tr,tc->rc", dt_low, d_dt_rounded, preferred_element_type=jnp.float32
    )
    d_dt_low = jnp.einsum("tc,rc->tr", d_dt_rounded, dt_weight, preferred_element_type=jnp.float32)
    d_pieces = lax.psum(
        jnp.concatenate([d_dt_low, jnp.sum(db_part, axis=2), jnp.sum(dc_part, axis=2)], axis=1),
        "tensor",
    ).astype(jnp.bfloat16)
    xproj_grad = jnp.einsum("tc,tk->ck", conv_out, d_pieces, preferred_element_type=jnp.float32)
    d_conv = (
        d_scanned * skip_gain
        + step_size * b_weighted
        + jnp.einsum("tk,ck->tc", d_pieces, xproj_weight, preferred_element_type=jnp.float32)
    )
    d_conv_pre = d_conv * silu_slope(conv_pre)
    conv_bias_grad = jnp.sum(d_conv_pre, axis=0)
    conv_taps = conv_weight.shape[0]
    tap_grads = []
    d_inner = jnp.zeros_like(inner_part)
    for distance in range(conv_taps):
        valid_grad = d_conv_pre * (offset >= distance).astype(jnp.float32)[:, None]
        tap_grads.append(jnp.sum(valid_grad * shift_down(inner_part, distance), axis=0))
        d_inner = d_inner + conv_weight[conv_taps - 1 - distance][None, :] * shift_up(
            valid_grad, distance
        )
    conv_weight_grad = jnp.stack(tap_grads[::-1], axis=0)
    d_projected = jnp.concatenate([d_inner, d_gate_z], axis=1).astype(jnp.bfloat16)
    d_projected_all = gather_rows(d_projected)
    d_normed = lax.psum(
        jnp.einsum("tk,dk->td", d_projected, in_flat, preferred_element_type=jnp.float32), "tensor"
    )
    gain_mixer_grad = jnp.sum(d_normed * owned_rows * scale_mixer, axis=0)
    d_tokens = d_hidden_in + rms_back(d_normed * norm_gain_mixer, owned_rows, scale_mixer)

    back_select = one_hot_rows(rank_within(arrival_index), row_count)
    arrive_select = jnp.transpose(one_hot_rows(slots_of(owner_index, row_count, share), row_count))
    output = pick_rows(arrive_select, exchange(pick_rows(back_select, output_own)))
    tokens_grad = pick_rows(
        arrive_select, exchange(pick_rows(back_select, d_tokens.astype(jnp.bfloat16)))
    )

    share_width = model_width // n_dp

    def my_columns(values):
        return lax.dynamic_slice_in_dim(values, me * share_width, share_width, axis=1)

    hidden_all, d_gate_all, d_up_all = mlp_parts(normed_mlp_all, grad_all)
    grad_cols = my_columns(grad_all)
    down_grad = jnp.einsum("tf,td->fd", hidden_all, grad_cols, preferred_element_type=jnp.float32)
    mlp_cols = my_columns(normed_mlp_all)

    def weight_grad(rows, upstream_rows):
        return jnp.einsum("td,tk->dk", rows, upstream_rows, preferred_element_type=jnp.float32)

    gate_up_grad = jnp.stack(
        [weight_grad(mlp_cols, d_gate_all), weight_grad(mlp_cols, d_up_all)], axis=1
    )
    out_grad = jnp.einsum("tc,td->cd", gated_all, d_mixed_cols, preferred_element_type=jnp.float32)
    in_grad = weight_grad(normed_cols, d_projected_all).reshape(share_width, 2, inner_width)

    def for_peers(values, axis):
        if values.ndim == 1:
            return values.reshape(n_dp, 1, -1)
        if axis == 0:
            return values.reshape(n_dp, values.shape[0] // n_dp, values.shape[1])
        return values.reshape(values.shape[0], n_dp, -1).transpose(1, 0, 2)

    small = [
        (gain_mixer_grad, 0),
        (conv_weight_grad, 1),
        (conv_bias_grad, 0),
        (xproj_grad, 0),
        (dt_weight_grad, 0),
        (dt_bias_grad, 0),
        (a_log_grad, 1),
        (skip_grad, 0),
        (gain_mlp_grad, 0),
    ]
    blocks = [for_peers(values, axis) for values, axis in small]
    packed = jnp.concatenate([block.reshape(n_dp, -1) for block in blocks], axis=1)
    summed = jnp.sum(exchange(packed), axis=0)
    results = []
    start = 0
    for (values, _), block in zip(small, blocks):
        size = block.shape[1] * block.shape[2]
        piece = summed[start : start + size]
        results.append(piece if values.ndim == 1 else piece.reshape(block.shape[1:]))
        start += size
    return (
        output,
        tokens_grad,
        results[0],
        in_grad,
        results[1],
        results[2],
        results[3],
        results[4],
        results[5],
        results[6],
        results[7],
        out_grad,
        results[8],
        gate_up_grad,
        down_grad,
    )


def solution(mesh):
    in_specs = (
        P("dp", None),
        P("dp", None),
        P("dp", None),
        P("dp"),
        P("dp"),
        P(),
        P(None, None, "tensor"),
        P(None, "tensor"),
        P("tensor"),
        P("tensor", None),
        P(None, "tensor"),
        P("tensor"),
        P(None, "tensor"),
        P("tensor"),
        P("tensor", None),
        P(),
        P(None, None, "tensor"),
        P("tensor", None),
    )
    out_specs = (
        P("dp", None),
        P("dp", None),
        P("dp"),
        P("dp", None, "tensor"),
        P(None, ("tensor", "dp")),
        P(("tensor", "dp")),
        P(("tensor", "dp"), None),
        P("dp", "tensor"),
        P(("tensor", "dp")),
        P(None, ("tensor", "dp")),
        P(("tensor", "dp")),
        P("tensor", "dp"),
        P("dp"),
        P("dp", None, "tensor"),
        P("tensor", "dp"),
    )
    step = functools.partial(body, n_dp=mesh.shape["dp"])
    return jax.shard_map(step, mesh=mesh, in_specs=in_specs, out_specs=out_specs, check_vma=False)
```
